32 devices in a mesh: wide: 8 (over z, y), narrow: 4 (over x, core).
Axes of the slice: x: 2, y: 2, z: 4, core: 2. Of those that a mesh axis runs over, the one named last changes fastest.
Arguments:
- entry_factor: bfloat16 [288, 4, 64, 1024], P('wide', 'narrow'), may hold values from -6 to 6
- entry_panel: int32 [288, 4], P('wide', 'narrow'), may hold values from 0 to 1
- entry_target: int32 [288, 4], P('wide', 'narrow'), may hold values from 0 to 7, as said below
- entry_count: int32 [4, 8], P('narrow', 'wide'), may hold values from 1 to 36, 96 in all within a row
- panel_shared: bfloat16 [16, 64, 1024], P('wide', None, 'narrow'), may hold values from -0.1875 to 0.1875
- coupling: float32 [16, 64, 64], P('wide'), may hold values from -0.75 to 0.75
- probes: bfloat16 [32, 64, 1024], P('narrow'), may hold values from -6 to 6
Outputs:
- left_factor: float32 [32, 64, 1024], P('narrow', None, 'wide')
- right_factor: float32 [32, 64, 1024], P('narrow', None, 'wide')
The draws below stay inside these ranges and needn't reach their ends.
Inputs may be any that keep to these rules, and one draw needn't show every extreme that they name: `entry_panel`: the local panel of an entry of any slot, live or not. `entry_target`: the local target of an entry; every target has at least one live entry. `entry_count`: the live slots of one device; for every owner the counts over the 8 wide indices sum to 96, and some device holds exactly 36.
All inputs are finite; a program needn't handle non-finite values.
Results may differ from the reference program's by a relative error of at most 0.0036.
Values may be sent and summed in bfloat16 or wider, within the bound.
A program may use at most 64 MiB of HBM per device.

```python
import math
import jax
import jax.numpy as jnp
import numpy as np
from jax import lax

B = 1024
R = 64
TGT_DEV = 8
DESC_DEV = 2
ENT_MEAN = 12
LIST_DEV = 36
OWNERS = 4
GROUPS = 8
TGT = 32
PANELS = 16
ENTRIES = 288
N_WIDE = 8


def draw_entry_target(key, part):
    row_index = jnp.arange(ENTRIES, dtype=jnp.int32)[:, None]
    owner_index = jnp.arange(OWNERS, dtype=jnp.int32)[None, :]
    random_target = jax.random.randint(key, (ENTRIES, OWNERS), 0, TGT_DEV, dtype=jnp.int32)
    first_target = (row_index // LIST_DEV + owner_index) % TGT_DEV
    return jnp.where(row_index % LIST_DEV == 0, first_target, random_target).astype(jnp.int32)


def touch_ends(drawn, rng, least, high):
    shape = drawn.shape
    index_at = [jax.random.randint(jax.random.fold_in(rng, axis), (), 0, shape[axis]) for axis in range(len(shape))]
    drawn = drawn.at[tuple(index_at)].set(least)
    longest = shape.index(max(shape))
    index_at[longest] = (index_at[longest] + 1) % shape[longest]
    return drawn.at[tuple(index_at)].set(high)


def steps_of(own_key, shape, cuts, least, largest):
    level = 1.0
    for axis_at, blocks in cuts:
        draws = jax.random.uniform(jax.random.fold_in(jax.random.fold_in(own_key, 6), axis_at), (blocks,), jnp.float32, least / len(cuts), largest / len(cuts))
        level = level * jnp.repeat(jnp.exp(draws), shape[axis_at] // blocks).reshape((-1,) + (1,) * (len(shape) - 1 - axis_at))
    return level


def length_profile(count, total, bound, lean):
    loads = [(1 << 20) // math.isqrt(standing ** lean) + 1 for standing in range(2, count + 1)]
    rest, given = total - bound - (count - 1), [1] * (count - 1)
    while rest > 0:
        free = [i for i in range(count - 1) if given[i] < bound]
        whole, left = sum([loads[i] for i in free]), rest
        for i in free:
            addition = min(bound - given[i], max(1, left * loads[i] // whole), rest)
            given[i] = given[i] + addition
            rest = rest - addition
    return np.array([bound] + given)


def ragged_sizes(own_key, number_of, total, bound, lean):
    if number_of == 2:
        one = jax.random.randint(own_key, (), max(1, total - bound), min(bound, total - 1) + 1)
        return jnp.stack([one, total - one])
    tallies = jnp.asarray(length_profile(number_of, total, bound, lean), jnp.int32)
    pairs = (number_of - 1) // 2
    giver, taker = tallies[1:1 + 2 * pairs:2], tallies[2:2 + 2 * pairs:2]
    margin = jnp.minimum(giver - 1, bound - taker)
    moved = jax.random.randint(jax.random.fold_in(own_key, 1), (pairs,), 0, 1 << 20) % (margin + 1)
    tallies = tallies.at[1:1 + 2 * pairs:2].set(giver - moved).at[2:2 + 2 * pairs:2].set(taker + moved)
    return tallies[jax.random.permutation(jax.random.fold_in(own_key, 2), number_of)]


def centred(stream_key, extent, scale, reach, shards=(), kind=jnp.bfloat16):
    array = jax.random.normal(stream_key, extent, jnp.float32) * scale
    if len(shards) > 0:
        array = steps_of(stream_key, extent, shards, -0.22, 0.18) * array
    return jnp.clip(array, min=-reach, max=reach).astype(kind)


def setup_inputs(seed: int = 0) -> dict:
    seeds = jax.random.split(jax.random.key(seed), 8)
    return {
        "entry_factor": centred(seeds[0], (ENTRIES, OWNERS, R, B), 1.0, 6.0, ((0, 8), (1, 4))),
        "entry_panel": touch_ends(jax.random.randint(seeds[1], (ENTRIES, OWNERS), 0, DESC_DEV), jax.random.fold_in(seeds[1], 1), 0, DESC_DEV - 1).astype(jnp.int32),
        "entry_target": draw_entry_target(jax.random.fold_in(seeds[7], 71), 0),
        "entry_count": jax.vmap(lambda own: ragged_sizes(own, GROUPS, ENT_MEAN * N_WIDE, LIST_DEV, 2))(jax.random.split(seeds[3], OWNERS)).reshape((OWNERS, GROUPS)).astype(jnp.int32),
        "panel_shared": centred(seeds[4], (PANELS, R, B), B ** -0.5, 0.1875, ((0, 8), (2, 4))),
        "coupling": centred(seeds[5], (PANELS, R, R), R ** -0.5, 0.75, ((0, 8),), jnp.float32),
        "probes": centred(seeds[6], (TGT, R, B), 1.0, 6.0, ((0, 4),)),
    }


def rounded(value):
    return lax.optimization_barrier(value.astype(jnp.bfloat16)).astype(jnp.float32)

def reference(entry_factor, entry_panel, entry_target, entry_count, panel_shared, coupling, probes):
    highest = lax.Precision.HIGHEST
    owner_count = entry_factor.shape[1]
    rank_dim = entry_factor.shape[2]
    full_width = entry_factor.shape[3]
    slot_ids = jnp.arange(LIST_DEV, dtype=jnp.int32)
    panel_ids = jnp.arange(DESC_DEV, dtype=jnp.int32)
    target_ids = jnp.arange(TGT_DEV, dtype=jnp.int32)
    probe_blocks = probes.astype(jnp.float32).reshape(owner_count, TGT_DEV, rank_dim, full_width)

    def group_data(group_index):
        entry_start = (group_index * LIST_DEV).astype(jnp.int32)
        factors = lax.dynamic_slice_in_dim(entry_factor, entry_start, LIST_DEV, 0).astype(jnp.float32)
        panels = lax.dynamic_slice_in_dim(entry_panel, entry_start, LIST_DEV, 0)
        targets = lax.dynamic_slice_in_dim(entry_target, entry_start, LIST_DEV, 0)
        counts = lax.dynamic_index_in_dim(entry_count, group_index, 1, keepdims=False)
        live_mask = (slot_ids[:, None] < counts[None, :]).astype(jnp.float32)
        pick_panel = (panels[:, :, None] == panel_ids[None, None, :]).astype(jnp.float32) * live_mask[:, :, None]
        pick_target = (targets[:, :, None] == target_ids[None, None, :]).astype(jnp.float32)
        panel_start = (group_index * DESC_DEV).astype(jnp.int32)
        shared = lax.dynamic_slice_in_dim(panel_shared, panel_start, DESC_DEV, 0).astype(jnp.float32)
        middle = lax.dynamic_slice_in_dim(coupling, panel_start, DESC_DEV, 0).astype(jnp.float32)
        return (factors, pick_panel, pick_target, shared, middle)

    def first_pass(sketch, group_index):
        factors, pick_panel, pick_target, shared, middle = group_data(group_index)
        projected = jnp.einsum('drb,otkb->dotrk', shared, probe_blocks, precision=highest)
        coefficients = rounded(jnp.einsum('dij,dotjk->dotik', middle, projected, precision=highest))
        weights = jnp.einsum('lod,lot->lodt', pick_panel, pick_target)
        chosen = jnp.einsum('lodt,dotik->loik', weights, coefficients, precision=highest)
        contributions = jnp.einsum('loji,lojb->loib', chosen, factors, precision=highest)
        return (sketch + jnp.einsum('lot,loib->otib', pick_target, contributions, precision=highest), None)
    zeros = jnp.zeros((owner_count, TGT_DEV, rank_dim, full_width), jnp.float32)
    group_list = jnp.arange(GROUPS, dtype=jnp.int32)
    sketch, _ = lax.scan(first_pass, zeros, group_list)
    gram_matrix = jnp.einsum('otib,otjb->otij', sketch, sketch, precision=highest)
    lower_factor = jnp.linalg.cholesky(gram_matrix)
    basis = lax.linalg.triangular_solve(lower_factor, sketch, left_side=True, lower=True)
    basis_round = rounded(basis)

    def second_pass(coeff_rows, group_index):
        factors, pick_panel, pick_target, shared, middle = group_data(group_index)
        selected = jnp.einsum('lot,otkb->lokb', pick_target, basis_round, precision=highest)
        back_terms = jnp.einsum('loib,lokb->loik', factors, selected, precision=highest)
        weights = jnp.einsum('lod,lot->lodt', pick_panel, pick_target)
        summed = jnp.einsum('lodt,loik->dotik', weights, back_terms, precision=highest)
        middle_terms = jnp.einsum('dotik,dij->dotkj', summed, middle, precision=highest)
        return (coeff_rows + jnp.einsum('dotkj,djb->otkb', middle_terms, shared, precision=highest), None)
    coeff_rows, _ = lax.scan(second_pass, zeros, group_list)
    root_width = math.sqrt(full_width)
    left_factor = (basis * root_width).reshape(TGT, rank_dim, full_width)
    right_factor = (coeff_rows / root_width).reshape(TGT, rank_dim, full_width)
    return (left_factor, right_factor)
```

```python
import math

import jax
import jax.numpy as jnp
from jax import lax
from jax.sharding import PartitionSpec as P


def shards(entry_factor, entry_panel, entry_target, entry_count, panel_shared, coupling, probes):
    highest = lax.Precision.HIGHEST
    factors = entry_factor[:, 0]
    slot_count = factors.shape[0]
    rank_dim = factors.shape[1]
    full_width = factors.shape[2]
    panel_count = panel_shared.shape[0]
    target_count = probes.shape[0]
    live_mask = (jnp.arange(slot_count) < entry_count[0, 0]).astype(jnp.float32)
    pick_panel = (entry_panel == jnp.arange(panel_count)[None, :]).astype(jnp.float32) * live_mask[
        :, None
    ]
    pick_target = (entry_target == jnp.arange(target_count)[None, :]).astype(jnp.float32)
    pair_pick = (pick_panel[:, :, None] * pick_target[:, None, :]).reshape(
        slot_count, panel_count * target_count
    )
    gathered = lax.all_gather(panel_shared, "narrow", axis=2, tiled=True)
    projected = jnp.einsum("drb,tkb->dtrk", gathered, probes, preferred_element_type=jnp.float32)
    coefficients = jnp.einsum("dij,dtjk->dtik", coupling, projected, precision=highest).astype(
        jnp.bfloat16
    )
    coeff_table = coefficients.reshape(panel_count * target_count, rank_dim * rank_dim)
    chosen = jnp.dot(
        pair_pick.astype(jnp.bfloat16), coeff_table, preferred_element_type=jnp.float32
    )
    chosen = chosen.astype(jnp.bfloat16).reshape(slot_count, rank_dim, rank_dim)
    contributions = jnp.einsum("eji,ejb->eib", chosen, factors, preferred_element_type=jnp.float32)
    sketch = jnp.einsum("et,eib->tib", pick_target, contributions, precision=highest)
    wide_count = lax.axis_size("wide")
    share_cols = full_width // wide_count
    sketch_part = lax.psum_scatter(sketch, "wide", scatter_dimension=2, tiled=True)
    gram_part = jnp.einsum("tib,tjb->tij", sketch_part, sketch_part, precision=highest)
    gram_matrix = lax.psum(gram_part, "wide")
    lower_factor = jnp.linalg.cholesky(gram_matrix)
    own_basis = jax.scipy.linalg.solve_triangular(lower_factor, sketch_part, lower=True)
    basis_round = lax.all_gather(own_basis.astype(jnp.bfloat16), "wide", axis=2, tiled=True)
    selected = jnp.einsum(
        "et,tkb->ekb",
        pick_target.astype(jnp.bfloat16),
        basis_round,
        preferred_element_type=jnp.float32,
    )
    selected = selected.astype(jnp.bfloat16)
    back_terms = jnp.einsum("eib,ekb->eik", factors, selected, preferred_element_type=jnp.float32)
    summed = jnp.einsum("ep,eik->pik", pair_pick, back_terms, precision=highest)
    summed = summed.reshape(panel_count, target_count, rank_dim, rank_dim)
    middle_terms = jnp.einsum("dtik,dij->dtkj", summed, coupling, precision=highest)
    partial_rows = jnp.einsum(
        "dtkj,djb->tkb", middle_terms, gathered.astype(jnp.float32), precision=highest
    )
    coeff_part = lax.psum_scatter(partial_rows, "wide", scatter_dimension=2, tiled=True)
    root_width = math.sqrt(full_width)
    return (own_basis * root_width, coeff_part / root_width)


def solution(mesh):
    placed = (
        P("wide", "narrow", None, None),
        P("wide", "narrow"),
        P("wide", "narrow"),
        P("narrow", "wide"),
        P("wide", None, "narrow"),
        P("wide", None, None),
        P("narrow", None, None),
    )
    return jax.shard_map(
        shards,
        mesh=mesh,
        in_specs=placed,
        out_specs=(P("narrow", None, "wide"), P("narrow", None, "wide")),
        check_vma=False,
    )
```

```python
import math

import jax
import jax.numpy as jnp
from jax import lax
from jax.sharding import PartitionSpec as P


def wide_reduce(x, count):
    lead, rows, width = x.shape
    pieces = x.reshape(lead, rows, count, width // count).transpose(2, 0, 1, 3)
    pieces = lax.all_to_all(pieces, "wide", 0, 0, tiled=True)
    return pieces.sum(axis=0)


def wide_gather(x, count):
    lead, rows, width = x.shape
    copies = jnp.broadcast_to(x[None], (count, lead, rows, width))
    copies = lax.all_to_all(copies, "wide", 0, 0, tiled=True)
    return copies.transpose(1, 2, 0, 3).reshape(lead, rows, count * width)


def shards(entry_factor, entry_panel, entry_target, entry_count, panel_shared, coupling, probes):
    highest = lax.Precision.HIGHEST
    factors = entry_factor[:, 0]
    slot_count = factors.shape[0]
    rank_dim = factors.shape[1]
    full_width = factors.shape[2]
    panel_count = panel_shared.shape[0]
    target_count = probes.shape[0]
    live_mask = (jnp.arange(slot_count) < entry_count[0, 0]).astype(jnp.float32)
    pick_panel = (entry_panel == jnp.arange(panel_count)[None, :]).astype(jnp.float32) * live_mask[
        :, None
    ]
    pick_target = (entry_target == jnp.arange(target_count)[None, :]).astype(jnp.float32)
    pair_pick = (pick_panel[:, :, None] * pick_target[:, None, :]).reshape(
        slot_count, panel_count * target_count
    )
    gathered = lax.all_gather(panel_shared, "narrow", axis=2, tiled=True)
    projected = jnp.einsum("drb,tkb->dtrk", gathered, probes, preferred_element_type=jnp.float32)
    coefficients = jnp.einsum("dij,dtjk->dtik", coupling, projected, precision=highest).astype(
        jnp.bfloat16
    )
    coeff_table = coefficients.reshape(panel_count * target_count, rank_dim * rank_dim)
    chosen = jnp.dot(
        pair_pick.astype(jnp.bfloat16), coeff_table, preferred_element_type=jnp.float32
    )
    chosen = chosen.astype(jnp.bfloat16).reshape(slot_count, rank_dim, rank_dim)
    contributions = jnp.einsum("eji,ejb->eib", chosen, factors, preferred_element_type=jnp.float32)
    sketch = jnp.einsum("et,eib->tib", pick_target, contributions, precision=highest)
    wide_count = lax.axis_size("wide")
    share_cols = full_width // wide_count
    sketch_sum = wide_gather(wide_reduce(sketch, wide_count), wide_count)
    gram_matrix = jnp.einsum("tib,tjb->tij", sketch_sum, sketch_sum, precision=highest)
    lower_factor = jnp.linalg.cholesky(gram_matrix)
    basis = jax.scipy.linalg.solve_triangular(lower_factor, sketch_sum, lower=True)
    basis_round = basis.astype(jnp.bfloat16)
    own_basis = lax.dynamic_slice_in_dim(basis, lax.axis_index("wide") * share_cols, share_cols, 2)
    selected = jnp.einsum(
        "et,tkb->ekb",
        pick_target.astype(jnp.bfloat16),
        basis_round,
        preferred_element_type=jnp.float32,
    )
    selected = selected.astype(jnp.bfloat16)
    back_terms = jnp.einsum("eib,ekb->eik", factors, selected, preferred_element_type=jnp.float32)
    summed = jnp.einsum("ep,eik->pik", pair_pick, back_terms, precision=highest)
    summed = summed.reshape(panel_count, target_count, rank_dim, rank_dim)
    middle_terms = jnp.einsum("dtik,dij->dtkj", summed, coupling, precision=highest)
    partial_rows = jnp.einsum(
        "dtkj,djb->tkb", middle_terms, gathered.astype(jnp.float32), precision=highest
    )
    coeff_part = wide_reduce(partial_rows, wide_count)
    root_width = math.sqrt(full_width)
    return (own_basis * root_width, coeff_part / root_width)


def solution(mesh):
    placed = (
        P("wide", "narrow", None, None),
        P("wide", "narrow"),
        P("wide", "narrow"),
        P("narrow", "wide"),
        P("wide", None, "narrow"),
        P("wide", None, None),
        P("narrow", None, None),
    )
    return jax.shard_map(
        shards,
        mesh=mesh,
        in_specs=placed,
        out_specs=(P("narrow", None, "wide"), P("narrow", None, "wide")),
        check_vma=False,
    )
```

```python
import math

import jax
import jax.numpy as jnp
from jax import lax
from jax.sharding import PartitionSpec as P


def wide_reduce(x, count):
    lead, rows, width = x.shape
    pieces = x.reshape(lead, rows, count, width // count).transpose(2, 0, 1, 3)
    pieces = lax.all_to_all(pieces, "wide", 0, 0, tiled=True)
    return pieces.sum(axis=0)


def wide_gather(x, count):
    lead, rows, width = x.shape
    copies = jnp.broadcast_to(x[None], (count, lead, rows, width))
    copies = lax.all_to_all(copies, "wide", 0, 0, tiled=True)
    return copies.transpose(1, 2, 0, 3).reshape(lead, rows, count * width)


def lower_inverse(lower):
    highest = lax.Precision.HIGHEST
    size = lower.shape[-1]
    eye = jnp.eye(size, dtype=lower.dtype)
    diag = jnp.diagonal(lower, axis1=-2, axis2=-1)
    strict = eye - lower / diag[..., :, None]
    unit_inverse = eye + strict
    power = strict
    for _ in range(max(size - 1, 1).bit_length() - 1):
        power = jnp.einsum("tij,tjk->tik", power, power, precision=highest)
        unit_inverse = unit_inverse + jnp.einsum(
            "tij,tjk->tik", unit_inverse, power, precision=highest
        )
    return unit_inverse / diag[..., None, :]


def shards(entry_factor, entry_panel, entry_target, entry_count, panel_shared, coupling, probes):
    highest = lax.Precision.HIGHEST
    factors = entry_factor[:, 0]
    slot_count = factors.shape[0]
    rank_dim = factors.shape[1]
    full_width = factors.shape[2]
    panel_count = panel_shared.shape[0]
    target_count = probes.shape[0]
    live_mask = (jnp.arange(slot_count) < entry_count[0, 0]).astype(jnp.float32)
    pick_panel = (entry_panel == jnp.arange(panel_count)[None, :]).astype(jnp.float32) * live_mask[
        :, None
    ]
    pick_target = (entry_target == jnp.arange(target_count)[None, :]).astype(jnp.float32)
    pair_pick = (pick_panel[:, :, None] * pick_target[:, None, :]).reshape(
        slot_count, panel_count * target_count
    )
    gathered = lax.all_gather(panel_shared, "narrow", axis=2, tiled=True)
    projected = jnp.einsum("drb,tkb->dtrk", gathered, probes, preferred_element_type=jnp.float32)
    coefficients = jnp.einsum("dij,dtjk->dtik", coupling, projected, precision=highest).astype(
        jnp.bfloat16
    )
    coeff_table = coefficients.reshape(panel_count * target_count, rank_dim * rank_dim)
    chosen = jnp.dot(
        pair_pick.astype(jnp.bfloat16), coeff_table, preferred_element_type=jnp.float32
    )
    chosen = chosen.astype(jnp.bfloat16).reshape(slot_count, rank_dim, rank_dim)
    contributions = jnp.einsum("eji,ejb->eib", chosen, factors, preferred_element_type=jnp.float32)
    sketch = jnp.einsum("et,eib->tib", pick_target, contributions, precision=highest)
    wide_count = lax.axis_size("wide")
    share_cols = full_width // wide_count
    sketch_sum = wide_gather(wide_reduce(sketch, wide_count), wide_count)
    gram_matrix = jnp.einsum("tib,tjb->tij", sketch_sum, sketch_sum, precision=highest)
    lower_factor = jnp.linalg.cholesky(gram_matrix)
    basis = jnp.einsum(
        "tij,tjb->tib", lower_inverse(lower_factor), sketch_sum, precision=highest
    )
    basis_round = basis.astype(jnp.bfloat16)
    own_basis = lax.dynamic_slice_in_dim(basis, lax.axis_index("wide") * share_cols, share_cols, 2)
    selected = jnp.einsum(
        "et,tkb->ekb",
        pick_target.astype(jnp.bfloat16),
        basis_round,
        preferred_element_type=jnp.float32,
    )
    selected = selected.astype(jnp.bfloat16)
    back_terms = jnp.einsum("eib,ekb->eik", factors, selected, preferred_element_type=jnp.float32)
    summed = jnp.einsum("ep,eik->pik", pair_pick, back_terms, precision=highest)
    summed = summed.reshape(panel_count, target_count, rank_dim, rank_dim)
    middle_terms = jnp.einsum("dtik,dij->dtkj", summed, coupling, precision=highest)
    partial_rows = jnp.einsum(
        "dtkj,djb->tkb", middle_terms, gathered.astype(jnp.float32), precision=highest
    )
    coeff_part = wide_reduce(partial_rows, wide_count)
    root_width = math.sqrt(full_width)
    return (own_basis * root_width, coeff_part / root_width)


def solution(mesh):
    placed = (
        P("wide", "narrow", None, None),
        P("wide", "narrow"),
        P("wide", "narrow"),
        P("narrow", "wide"),
        P("wide", None, "narrow"),
        P("wide", None, None),
        P("narrow", None, None),
    )
    return jax.shard_map(
        shards,
        mesh=mesh,
        in_specs=placed,
        out_specs=(P("narrow", None, "wide"), P("narrow", None, "wide")),
        check_vma=False,
    )
```

```python
import math

import jax
import jax.numpy as jnp
from jax import lax
from jax.sharding import PartitionSpec as P


def wide_reduce(x, count):
    lead, rows, width = x.shape
    pieces = x.reshape(lead, rows, count, width // count).transpose(2, 0, 1, 3)
    pieces = lax.all_to_all(pieces, "wide", 0, 0, tiled=True)
    return pieces.sum(axis=0)


def wide_gather(x, count):
    lead, rows, width = x.shape
    copies = jnp.broadcast_to(x[None], (count, lead, rows, width))
    copies = lax.all_to_all(copies, "wide", 0, 0, tiled=True)
    return copies.transpose(1, 2, 0, 3).reshape(lead, rows, count * width)


def lower_inverse(lower):
    highest = lax.Precision.HIGHEST
    size = lower.shape[-1]
    eye = jnp.eye(size, dtype=lower.dtype)
    diag = jnp.diagonal(lower, axis1=-2, axis2=-1)
    strict = eye - lower / diag[..., :, None]
    unit_inverse = eye + strict
    power = strict
    for _ in range(max(size - 1, 1).bit_length() - 1):
        power = jnp.einsum("tij,tjk->tik", power, power, precision=highest)
        unit_inverse = unit_inverse + jnp.einsum(
            "tij,tjk->tik", unit_inverse, power, precision=highest
        )
    return unit_inverse / diag[..., None, :]


def shards(entry_factor, entry_panel, entry_target, entry_count, panel_shared, coupling, probes):
    highest = lax.Precision.HIGHEST
    factors = entry_factor[:, 0]
    slot_count = factors.shape[0]
    rank_dim = factors.shape[1]
    full_width = factors.shape[2]
    panel_count = panel_shared.shape[0]
    target_count = probes.shape[0]
    live_mask = (jnp.arange(slot_count) < entry_count[0, 0]).astype(jnp.float32)
    pick_panel = (entry_panel == jnp.arange(panel_count)[None, :]).astype(jnp.float32) * live_mask[
        :, None
    ]
    pick_target = (entry_target == jnp.arange(target_count)[None, :]).astype(jnp.float32)
    pair_pick = (pick_panel[:, :, None] * pick_target[:, None, :]).reshape(
        slot_count, panel_count * target_count
    )
    gathered = lax.all_gather(panel_shared, "narrow", axis=2, tiled=True)
    projected = jnp.einsum("drb,tkb->dtrk", gathered, probes, preferred_element_type=jnp.float32)
    coefficients = jnp.einsum("dij,dtjk->dtik", coupling, projected, precision=highest).astype(
        jnp.bfloat16
    )
    coeff_table = coefficients.reshape(panel_count * target_count, rank_dim * rank_dim)
    chosen = jnp.dot(
        pair_pick.astype(jnp.bfloat16), coeff_table, preferred_element_type=jnp.float32
    )
    chosen = chosen.astype(jnp.bfloat16).reshape(slot_count, rank_dim, rank_dim)
    contributions = jnp.einsum("eji,ejb->eib", chosen, factors, preferred_element_type=jnp.float32)
    sketch = jnp.einsum("et,eib->tib", pick_target, contributions, precision=highest)
    wide_count = lax.axis_size("wide")
    share_cols = full_width // wide_count
    sketch_own = wide_reduce(sketch, wide_count)
    gram_part = jnp.einsum("tib,tjb->tij", sketch_own, sketch_own, precision=highest)
    gram_copies = jnp.broadcast_to(gram_part[None], (wide_count,) + gram_part.shape)
    gram_matrix = lax.all_to_all(gram_copies, "wide", 0, 0, tiled=True).sum(axis=0)
    sketch_sum = wide_gather(sketch_own, wide_count)
    lower_factor = jnp.linalg.cholesky(gram_matrix)
    basis = jnp.einsum(
        "tij,tjb->tib", lower_inverse(lower_factor), sketch_sum, precision=highest
    )
    basis_round = basis.astype(jnp.bfloat16)
    own_basis = lax.dynamic_slice_in_dim(basis, lax.axis_index("wide") * share_cols, share_cols, 2)
    selected = jnp.einsum(
        "et,tkb->ekb",
        pick_target.astype(jnp.bfloat16),
        basis_round,
        preferred_element_type=jnp.float32,
    )
    selected = selected.astype(jnp.bfloat16)
    back_terms = jnp.einsum("eib,ekb->eik", factors, selected, preferred_element_type=jnp.float32)
    summed = jnp.einsum("ep,eik->pik", pair_pick, back_terms, precision=highest)
    summed = summed.reshape(panel_count, target_count, rank_dim, rank_dim)
    middle_terms = jnp.einsum("dtik,dij->dtkj", summed, coupling, precision=highest)
    partial_rows = jnp.einsum(
        "dtkj,djb->tkb", middle_terms, gathered.astype(jnp.float32), precision=highest
    )
    coeff_part = wide_reduce(partial_rows, wide_count)
    root_width = math.sqrt(full_width)
    return (own_basis * root_width, coeff_part / root_width)


def solution(mesh):
    placed = (
        P("wide", "narrow", None, None),
        P("wide", "narrow"),
        P("wide", "narrow"),
        P("narrow", "wide"),
        P("wide", None, "narrow"),
        P("wide", None, None),
        P("narrow", None, None),
    )
    return jax.shard_map(
        shards,
        mesh=mesh,
        in_specs=placed,
        out_specs=(P("narrow", None, "wide"), P("narrow", None, "wide")),
        check_vma=False,
    )
```

```python
import math

import jax
import jax.numpy as jnp
from jax import lax
from jax.sharding import PartitionSpec as P


def wide_reduce(x, count):
    lead, rows, width = x.shape
    pieces = x.reshape(lead, rows, count, width // count).transpose(2, 0, 1, 3)
    pieces = lax.all_to_all(pieces, "wide", 0, 0, tiled=True)
    return pieces.sum(axis=0)


def wide_gather(x, count):
    lead, rows, width = x.shape
    copies = jnp.broadcast_to(x[None], (count, lead, rows, width))
    copies = lax.all_to_all(copies, "wide", 0, 0, tiled=True)
    return copies.transpose(1, 2, 0, 3).reshape(lead, rows, count * width)


def lower_inverse(lower):
    highest = lax.Precision.HIGHEST
    size = lower.shape[-1]
    eye = jnp.eye(size, dtype=lower.dtype)
    diag = jnp.diagonal(lower, axis1=-2, axis2=-1)
    strict = eye - lower / diag[..., :, None]
    unit_inverse = eye + strict
    power = strict
    for _ in range(max(size - 1, 1).bit_length() - 1):
        power = jnp.einsum("tij,tjk->tik", power, power, precision=highest)
        unit_inverse = unit_inverse + jnp.einsum(
            "tij,tjk->tik", unit_inverse, power, precision=highest
        )
    return unit_inverse / diag[..., None, :]


def shards(entry_factor, entry_panel, entry_target, entry_count, panel_shared, coupling, probes):
    highest = lax.Precision.HIGHEST
    factors = entry_factor[:, 0]
    slot_count = factors.shape[0]
    rank_dim = factors.shape[1]
    full_width = factors.shape[2]
    panel_count = panel_shared.shape[0]
    target_count = probes.shape[0]
    live_mask = (jnp.arange(slot_count) < entry_count[0, 0]).astype(jnp.float32)
    pick_panel = (entry_panel == jnp.arange(panel_count)[None, :]).astype(jnp.float32) * live_mask[
        :, None
    ]
    pick_target = (entry_target == jnp.arange(target_count)[None, :]).astype(jnp.float32)
    pair_pick = (pick_panel[:, :, None] * pick_target[:, None, :]).reshape(
        slot_count, panel_count * target_count
    )
    gathered = lax.all_gather(panel_shared, "narrow", axis=2, tiled=True)
    projected = jnp.einsum("drb,tkb->dtrk", gathered, probes, preferred_element_type=jnp.float32)
    coefficients = jnp.einsum("dij,dtjk->dtik", coupling, projected, precision=highest).astype(
        jnp.bfloat16
    )
    coeff_table = coefficients.reshape(panel_count * target_count, rank_dim * rank_dim)
    chosen = jnp.dot(
        pair_pick.astype(jnp.bfloat16), coeff_table, preferred_element_type=jnp.float32
    )
    chosen = chosen.astype(jnp.bfloat16).reshape(slot_count, rank_dim, rank_dim)
    contributions = jnp.einsum("eji,ejb->eib", chosen, factors, preferred_element_type=jnp.float32)
    sketch = jnp.einsum("et,eib->tib", pick_target, contributions, precision=highest)
    wide_count = lax.axis_size("wide")
    share_cols = full_width // wide_count
    sketch_own = wide_reduce(sketch, wide_count)
    gram_part = jnp.einsum("tib,tjb->tij", sketch_own, sketch_own, precision=highest)
    gram_copies = jnp.broadcast_to(gram_part[None], (wide_count,) + gram_part.shape)
    gram_matrix = lax.all_to_all(gram_copies, "wide", 0, 0, tiled=True).sum(axis=0)
    sketch_sum = wide_gather(sketch_own, wide_count)
    lower_factor = jnp.linalg.cholesky(gram_matrix)
    basis = jnp.einsum(
        "tij,tjb->tib", lower_inverse(lower_factor), sketch_sum, precision=highest
    )
    basis_round = basis.astype(jnp.bfloat16)
    own_basis = lax.dynamic_slice_in_dim(basis, lax.axis_index("wide") * share_cols, share_cols, 2)
    selected = jnp.einsum(
        "et,tkb->ekb",
        pick_target.astype(jnp.bfloat16),
        basis_round,
        preferred_element_type=jnp.float32,
    )
    selected = selected.astype(jnp.bfloat16)
    back_terms = jnp.einsum("eib,ekb->eik", factors, selected, preferred_element_type=jnp.float32)
    summed = jnp.einsum("ep,eik->pik", pair_pick, back_terms, precision=highest)
    summed = summed.reshape(panel_count, target_count, rank_dim, rank_dim)
    middle_terms = jnp.einsum("dtik,dij->dtkj", summed, coupling, precision=highest)
    half = target_count // 2
    coeff_halves = []
    for lo, hi in ((0, half), (half, target_count)):
        partial_rows = jnp.einsum(
            "dtkj,djb->tkb",
            middle_terms[:, lo:hi],
            gathered.astype(jnp.float32),
            precision=highest,
        )
        coeff_halves.append(wide_reduce(partial_rows, wide_count))
    coeff_part = jnp.concatenate(coeff_halves, axis=0)
    root_width = math.sqrt(full_width)
    return (own_basis * root_width, coeff_part / root_width)


def solution(mesh):
    placed = (
        P("wide", "narrow", None, None),
        P("wide", "narrow"),
        P("wide", "narrow"),
        P("narrow", "wide"),
        P("wide", None, "narrow"),
        P("wide", None, None),
        P("narrow", None, None),
    )
    return jax.shard_map(
        shards,
        mesh=mesh,
        in_specs=placed,
        out_specs=(P("narrow", None, "wide"), P("narrow", None, "wide")),
        check_vma=False,
    )
```
